32 devices in a mesh: groups: 2 (over y), ctx: 16 (over z, x, core).
Axes of the slice: x: 2, y: 2, z: 4, core: 2. Of those that a mesh axis runs over, the one named last changes fastest.
Arguments:
- queries: bfloat16 [12288, 1024], P(('groups', 'ctx')), parts along dimension 0, may hold values from -14 to 14
- inputs: bfloat16 [12288, 1024], P(('groups', 'ctx')), parts along dimension 0, may hold values from -6 to 6
- w_kv: bfloat16 [1024, 2048], replicated, may hold values from -1 to 1
- rand_blocks: int32 [192, 3], P('groups'), parts along dimension 0, may hold values from 1 to 94, as said below
- w_cross: bfloat16 [1024, 2048], replicated, may hold values from -1 to 1
- vocab_table: bfloat16 [6144, 1024], P('ctx'), may hold values from -14 to 14
- summary_ids: int32 [512], P('groups'), parts along dimension 0, may hold values from 0 to 6143
Outputs:
- attended: bfloat16 [12288, 1024], P(('groups', 'ctx')), parts along dimension 0
- summary: bfloat16 [512, 1024], P(('groups', 'ctx')), parts along dimension 0
The draws below stay inside these ranges and needn't reach their ends.
There are 2 independent parts, one for each index of `groups`. The reference program is written for one: setup_inputs(seed, part) draws one part's arguments, and reference() takes and returns one part's arrays. A program takes and returns all parts, laid end to end along the dimension named above; an argument that names none is the same for every part. Nothing has to cross between parts.
Inputs may be any that keep to these rules, and one draw needn't show every extreme that they name: `rand_blocks`: take each run of 6 query blocks that starts at a multiple of 6: its 18 random blocks never lie in its own run (they may lie in any other run, and may repeat a block of the window), the 3 blocks of one query block lie in different runs, at most 2 of them lie in any one other run and some run holds exactly 2 of them. No random block is block 0 or block 95.
All inputs are finite; a program needn't handle non-finite values.
Results may differ from the reference program's by a relative error of at most 0.0075.
Values may be sent and summed in bfloat16 or wider, within the bound.
A program may use at most 192 MiB of HBM per device.

```python
import math
import jax
import jax.numpy as jnp
import numpy as np
from jax import lax

D = 1024
HEADS = 16
HEAD = 64
BLOCK = 64
RAND = 3
BLK_DEV = 6
SUM = 256
NBLOCKS = 96
SEQ = 6144
VOCAB = 6144
N_CTX = 16


def draw_queries(key, part):
    sub_key = jax.random.fold_in(key, 11)
    base_rows = jnp.clip(jax.random.normal(sub_key, (SEQ, D), jnp.float32), -6.0, 6.0)
    return base_rows.astype(jnp.bfloat16)


def draw_inputs(key, part):
    sub_key = jax.random.fold_in(key, 12)
    base_rows = jnp.clip(jax.random.normal(sub_key, (SEQ, D), jnp.float32), -6.0, 6.0)
    return base_rows.astype(jnp.bfloat16)


def projection_pair(key):
    noise = jax.random.normal(jax.random.fold_in(key, 1), (D, 2 * D), jnp.float32) * D ** (-0.5)
    matrix = noise
    return jnp.clip(matrix, -1.0, 1.0).astype(jnp.bfloat16)


def draw_w_kv(key, part):
    return projection_pair(jax.random.fold_in(key, 21))


def draw_w_cross(key, part):
    return projection_pair(jax.random.fold_in(key, 22))


def draw_vocab_table(key, part):
    sub_key = jax.random.fold_in(key, 31)
    base_rows = jnp.clip(jax.random.normal(sub_key, (VOCAB, D), jnp.float32), -6.0, 6.0)
    return base_rows.astype(jnp.bfloat16)


def draw_rand_blocks(key, part):
    request_count = RAND * BLK_DEV
    spare = N_CTX - 1
    reach = min(request_count, spare)

    def one_device(device_key, device_index):
        rest = jax.random.permutation(jax.random.fold_in(device_key, 1), spare - 1).astype(jnp.int32)
        forced = jax.random.randint(jax.random.fold_in(device_key, 3), (), 0, reach, dtype=jnp.int32)
        places = jnp.arange(spare, dtype=jnp.int32)
        shifted = rest[jnp.clip(places - 1, 0, spare - 2)]
        unshifted = rest[jnp.clip(places, 0, spare - 2)]
        order = jnp.where(places < forced, unshifted, jnp.where(places == forced, spare - 1, shifted)).astype(jnp.int32)
        slots = jnp.arange(request_count, dtype=jnp.int32) % spare
        owners = (device_index + 1 + order[slots]) % N_CTX
        lowest = jnp.where(owners == 0, 1, 0).astype(jnp.int32)
        highest = jnp.where(owners == N_CTX - 1, BLK_DEV - 1, BLK_DEV).astype(jnp.int32)
        within = jax.random.randint(jax.random.fold_in(device_key, 2), (request_count,), lowest, highest, dtype=jnp.int32)
        return (owners * BLK_DEV + within).reshape(BLK_DEV, RAND)
    device_keys = jax.random.split(jax.random.fold_in(key, 41), N_CTX)
    table = jax.vmap(one_device)(device_keys, jnp.arange(N_CTX, dtype=jnp.int32))
    return table.reshape(NBLOCKS, RAND).astype(jnp.int32)


def plant(values, key, least, high):
    place = [jax.random.randint(jax.random.fold_in(key, axis), (), 0, length) for axis, length in enumerate(values.shape)]
    longest = values.shape.index(max(values.shape))
    next_to = place[:longest] + [(place[longest] + 1) % values.shape[longest]] + place[longest + 1:]
    return values.at[tuple(place)].set(least).at[tuple(next_to)].set(high)


def rank_bounds(count, lean):
    weights = [(1 << 20) // math.isqrt(standing ** lean) + 1 for standing in range(1, count + 1)]
    spread = 1 + sum(weights) // (1 << 30)
    return np.cumsum(np.array([max(1, weight // spread) for weight in weights]))


def ranked(key, extent, number_of, lean):
    listing = rank_bounds(number_of, lean)
    ticket = jax.random.randint(jax.random.fold_in(key, 1), extent, 0, int(listing[number_of - 1]))
    standing = jnp.searchsorted(jnp.asarray(listing, jnp.int32), ticket, side="right")
    return jax.random.permutation(jax.random.fold_in(key, 2), number_of)[standing].astype(jnp.int32)


def setup_inputs(seed: int = 0, part: int = 0) -> dict:
    keys = jax.random.split(jax.random.key(seed), 8)
    part_keys = jax.random.split(jax.random.fold_in(keys[7], part), 8)
    queries = draw_queries(jax.random.fold_in(jax.random.fold_in(keys[7], part), 71), part)
    inputs = draw_inputs(jax.random.fold_in(jax.random.fold_in(keys[7], part), 71), part)
    w_kv = draw_w_kv(jax.random.fold_in(keys[7], 71), part)
    rand_blocks = draw_rand_blocks(jax.random.fold_in(jax.random.fold_in(keys[7], part), 71), part)
    w_cross = draw_w_cross(jax.random.fold_in(keys[7], 71), part)
    vocab_table = draw_vocab_table(jax.random.fold_in(keys[7], 71), part)
    summary_ids = plant(ranked(part_keys[6], (SUM,), VOCAB, 2), jax.random.fold_in(part_keys[6], 3), 0, VOCAB - 1).astype(jnp.int32)
    return {"queries": queries, "inputs": inputs, "w_kv": w_kv, "rand_blocks": rand_blocks, "w_cross": w_cross, "vocab_table": vocab_table, "summary_ids": summary_ids}


MASKED_SCORE = -1e30


def split_heads(block_rows):
    return block_rows.astype(jnp.float32).reshape(block_rows.shape[0], HEADS, HEAD)


def window_rows(query_rows, key_rows, value_rows, valid):
    scores = jnp.einsum("qhe,khe->hqk", split_heads(query_rows), split_heads(key_rows)) * (HEAD ** -0.5)
    scores = jnp.where(valid[None, None, :], scores, MASKED_SCORE)
    scores = scores - jnp.max(scores, axis=2, keepdims=True)
    weights = jnp.exp(scores)
    weights = (weights / jnp.sum(weights, axis=2, keepdims=True)).astype(jnp.bfloat16)
    result = jnp.einsum("hqk,khe->qhe", weights.astype(jnp.float32), split_heads(value_rows))
    return result.reshape(query_rows.shape[0], HEADS * HEAD)


def full_rows(query_rows, key_heads, value_heads):
    scores = jnp.einsum("qhe,khe->hqk", split_heads(query_rows), key_heads) * (HEAD ** -0.5)
    weights = jnp.exp(scores - jnp.max(scores, axis=2, keepdims=True))
    totals = jnp.sum(weights, axis=2)
    result = jnp.einsum("hqk,khe->qhe", weights, value_heads, precision=lax.Precision.HIGHEST)
    return (result / jnp.transpose(totals)[:, :, None]).reshape(query_rows.shape[0], HEADS * HEAD)


def reference(queries, inputs, w_kv, rand_blocks, w_cross, vocab_table, summary_ids):
    seq_rows, feature_count = inputs.shape
    block_total = seq_rows // BLOCK
    pick_count = rand_blocks.shape[1]
    key_value = jnp.dot(inputs, w_kv, preferred_element_type=jnp.float32).astype(jnp.bfloat16)
    key_blocks = key_value[:, :feature_count].reshape(block_total, BLOCK, feature_count)
    value_blocks = key_value[:, feature_count:].reshape(block_total, BLOCK, feature_count)
    query_blocks = queries.reshape(block_total, BLOCK, feature_count)
    always = jnp.ones((), dtype=bool)

    def one_block(block_index):
        near = jnp.stack([block_index - 1, block_index, block_index + 1, 0 * block_index, 0 * block_index + block_total - 1])
        chosen = jnp.concatenate([near.astype(jnp.int32), rand_blocks[block_index].astype(jnp.int32)])
        chosen = jnp.clip(chosen, 0, block_total - 1).astype(jnp.int32)
        flags = jnp.concatenate([jnp.stack([block_index >= 2, always, block_index <= block_total - 3, always, always]), jnp.ones((pick_count,), dtype=bool)])
        valid = jnp.repeat(flags, BLOCK)
        key_rows = key_blocks[chosen].reshape(-1, feature_count)
        value_rows = value_blocks[chosen].reshape(-1, feature_count)
        return window_rows(query_blocks[block_index], key_rows, value_rows, valid)

    def one_group(group_index):
        return jax.vmap(one_block)(group_index * BLK_DEV + jnp.arange(BLK_DEV, dtype=jnp.int32))

    group_count = block_total // BLK_DEV
    sparse_out = lax.map(one_group, jnp.arange(group_count, dtype=jnp.int32)).reshape(block_total, BLOCK, feature_count)
    key_heads = split_heads(key_value[:, :feature_count])
    value_heads = split_heads(key_value[:, feature_count:])
    first_rows = full_rows(query_blocks[0], key_heads, value_heads)
    last_rows = full_rows(query_blocks[block_total - 1], key_heads, value_heads)
    sparse_out = sparse_out.at[0].set(first_rows).at[block_total - 1].set(last_rows)
    attended = sparse_out.reshape(seq_rows, feature_count).astype(jnp.bfloat16)
    encoded = (inputs.astype(jnp.float32) + attended.astype(jnp.float32)).astype(jnp.bfloat16)
    cross = jnp.dot(encoded, w_cross, preferred_element_type=jnp.float32).astype(jnp.bfloat16)
    cross_keys = split_heads(cross[:, :feature_count])
    cross_values = split_heads(cross[:, feature_count:])
    summary_queries = vocab_table[summary_ids]
    summary_count = summary_queries.shape[0]

    def summary_block(query_rows):
        return full_rows(query_rows, cross_keys, cross_values)

    summary = lax.map(summary_block, summary_queries.reshape(summary_count // 16, 16, feature_count))
    summary = summary.reshape(summary_count, feature_count).astype(jnp.bfloat16)
    return (attended, summary)
```

```python
import functools

import jax
import jax.numpy as jnp
from jax import lax
from jax.experimental import pallas as pl
from jax.experimental.pallas import tpu as pltpu
from jax.sharding import PartitionSpec as P

HEADS = 16
HEAD = 64
BLOCK = 64
LANES = 128
PAIRS = HEADS // 2
MASKED_SCORE = -1e30
MESH = pl.DeviceIdType.MESH
VMEM = pl.BlockSpec(memory_space=pltpu.VMEM)
ANY = pl.BlockSpec(memory_space=pl.ANY)
SMEM = pl.BlockSpec(memory_space=pltpu.SMEM)
VMEM_LIMIT = 48 * 1024 * 1024


def exchange_kernel(n, count, same, *refs):
    sources = refs[:count]
    targets = refs[count : 2 * count]
    send_sem, recv_sem, own_sem = refs[2 * count :]
    me = lax.axis_index("ctx")

    def piece(ref, peer):
        return ref if same else ref.at[peer]

    barrier = pltpu.get_barrier_semaphore()

    def greet(k, carry):
        peer = lax.rem(me + k, n)
        pl.semaphore_signal(barrier, inc=1, device_id={"ctx": peer}, device_id_type=MESH)
        return carry

    lax.fori_loop(1, n, greet, 0)
    own = [
        pltpu.make_async_copy(piece(sources[i], me), targets[i].at[me], own_sem.at[i])
        for i in range(count)
    ]
    for copy in own:
        copy.start()
    pl.semaphore_wait(barrier, n - 1)

    def push(i, peer, slot):
        return pltpu.make_async_remote_copy(
            piece(sources[i], peer),
            targets[i].at[slot],
            send_sem.at[i, peer],
            recv_sem.at[i, slot],
            device_id={"ctx": peer},
            device_id_type=MESH,
        )

    def send(k, carry):
        peer = lax.rem(me + k, n)
        for i in range(count):
            push(i, peer, me).start()
        return carry

    lax.fori_loop(1, n, send, 0)

    def finish(k, carry):
        peer = lax.rem(me + n - k, n)
        for i in range(count):
            push(i, peer, peer).wait_recv()
            push(i, peer, peer).wait_send()
        return carry

    lax.fori_loop(1, n, finish, 0)
    for copy in own:
        copy.wait()


def exchange(arrays, collective_id, same=False):
    n = lax.axis_size("ctx")
    count = len(arrays)
    shapes = [((n,) + x.shape) if same else x.shape for x in arrays]
    return pl.pallas_call(
        functools.partial(exchange_kernel, n, count, same),
        out_shape=[jax.ShapeDtypeStruct(s, x.dtype) for s, x in zip(shapes, arrays)],
        in_specs=[ANY] * count,
        out_specs=[ANY] * count,
        scratch_shapes=[
            pltpu.SemaphoreType.DMA((count, n)),
            pltpu.SemaphoreType.DMA((count, n)),
            pltpu.SemaphoreType.DMA((count,)),
        ],
        compiler_params=pltpu.CompilerParams(collective_id=collective_id, has_side_effects=True),
        name=f"exchange_{collective_id}",
    )(*arrays)


def dot_t(a, b):
    return lax.dot_general(a, b, (((1,), (1,)), ((), ())), preferred_element_type=jnp.float32)


def stacked_pair(q):
    q = q * jnp.asarray(HEAD**-0.5, q.dtype)
    left = lax.broadcasted_iota(jnp.int32, q.shape, 1) < HEAD
    zero = jnp.zeros_like(q)
    return jnp.concatenate([jnp.where(left, q, zero), jnp.where(left, zero, q)], axis=0)


def unstacked_pair(o):
    rows = o.shape[0] // 2
    left = lax.broadcasted_iota(jnp.int32, (rows, LANES), 1) < HEAD
    return jnp.where(left, o[:rows], o[rows:])


def project(x_ref, w_ref, out_ref, tile):
    rows, cols = out_ref.shape
    width = 512

    def step(t, carry):
        at = pl.ds(pl.multiple_of(t * tile, tile), tile)
        x = x_ref[at, :]
        for c in range(cols // width):
            y = jnp.dot(
                x, w_ref[:, c * width : (c + 1) * width], preferred_element_type=jnp.float32
            )
            out_ref[at, c * width : (c + 1) * width] = y.astype(out_ref.dtype)
        return carry

    lax.fori_loop(0, rows // tile, step, 0)


def partial_attention(q_ref, kv_ref, out_ref, log_ref):
    rows, features = q_ref.shape
    place = lax.broadcasted_iota(jnp.int32, (rows, LANES), 1)
    logs = jnp.zeros((rows, LANES), jnp.float32)
    for p in range(PAIRS):
        lanes = slice(p * LANES, (p + 1) * LANES)
        values = slice(features + p * LANES, features + (p + 1) * LANES)
        scores = dot_t(stacked_pair(q_ref[:, lanes]), kv_ref[:, lanes])
        peak = jnp.max(scores, axis=1, keepdims=True)
        weights = jnp.exp(scores - peak)
        totals = jnp.sum(weights, axis=1, keepdims=True)
        sums = jnp.dot(
            weights.astype(jnp.bfloat16), kv_ref[:, values], preferred_element_type=jnp.float32
        )
        out_ref[:, lanes] = unstacked_pair(sums / totals).astype(out_ref.dtype)
        log = peak + jnp.log(totals)
        logs = jnp.where(place == 2 * p, log[:rows], logs)
        logs = jnp.where(place == 2 * p + 1, log[rows:], logs)
    log_ref[...] = logs


def global_kernel(q_ref, x_ref, w_ref, out_ref, log_ref, kv_ref):
    project(x_ref, w_ref, kv_ref, 128)
    partial_attention(q_ref, kv_ref, out_ref, log_ref)


def global_partial(q, x, w):
    return pl.pallas_call(
        global_kernel,
        out_shape=[
            jax.ShapeDtypeStruct(q.shape, jnp.bfloat16),
            jax.ShapeDtypeStruct((q.shape[0], LANES), jnp.float32),
        ],
        in_specs=[VMEM] * 3,
        out_specs=[VMEM] * 2,
        scratch_shapes=[pltpu.VMEM((x.shape[0], w.shape[1]), jnp.bfloat16)],
        compiler_params=pltpu.CompilerParams(vmem_limit_bytes=VMEM_LIMIT),
        cost_estimate=pl.CostEstimate(
            flops=2 * x.size * w.shape[1], bytes_accessed=6 << 20, transcendentals=1 << 20
        ),
        name="global_partial",
    )(q, x, w)


def block_kernel(
    pick_count,
    ids_ref,
    edge_ref,
    all_ref,
    q_ref,
    x_ref,
    w_kv_ref,
    w_cross_ref,
    ends_ref,
    sq_ref,
    attended_ref,
    out_ref,
    log_ref,
    rows_ref,
    kv_ref,
    sem,
):
    row_count, features = x_ref.shape
    block_count = row_count // BLOCK
    slots = rows_ref.shape[0] // BLOCK
    far_start = (block_count + 4) * BLOCK
    span = (5 + pick_count) * BLOCK

    def fetch(i):
        return pltpu.make_async_copy(
            all_ref.at[ids_ref[i]],
            rows_ref.at[pl.ds(pl.multiple_of(i * BLOCK, BLOCK), BLOCK)],
            sem.at[i],
        )

    for i in range(slots):
        fetch(i).start()
    for i in range(slots):
        fetch(i).wait()
    project(rows_ref, w_kv_ref, kv_ref, 2 * BLOCK)

    column = lax.broadcasted_iota(jnp.int32, (2 * BLOCK, span), 1)

    def one_block(b, carry):
        first = edge_ref[0] + b
        hidden = jnp.logical_or(
            jnp.logical_and(column < BLOCK, first < 2),
            jnp.logical_and(
                jnp.logical_and(column >= 2 * BLOCK, column < 3 * BLOCK), first > edge_ref[1] - 3
            ),
        )
        near = pl.ds(pl.multiple_of(b * BLOCK, BLOCK), 3 * BLOCK)
        ends = pl.ds((block_count + 2) * BLOCK, 2 * BLOCK)
        far = pl.ds(
            pl.multiple_of(far_start + b * pick_count * BLOCK, BLOCK), pick_count * BLOCK
        )
        here = pl.ds(pl.multiple_of(b * BLOCK, BLOCK), BLOCK)
        for p in range(PAIRS):
            lanes = slice(p * LANES, (p + 1) * LANES)
            values = slice(features + p * LANES, features + (p + 1) * LANES)
            k = jnp.concatenate(
                [kv_ref[near, lanes], kv_ref[ends, lanes], kv_ref[far, lanes]], axis=0
            )
            v = jnp.concatenate(
                [kv_ref[near, values], kv_ref[ends, values], kv_ref[far, values]], axis=0
            )
            scores = dot_t(stacked_pair(q_ref[here, lanes]), k)
            scores = jnp.where(hidden, MASKED_SCORE, scores)
            weights = jnp.exp(scores - jnp.max(scores, axis=1, keepdims=True))
            totals = jnp.sum(weights, axis=1, keepdims=True)
            probs = (weights * (1.0 / totals)).astype(jnp.bfloat16)
            o = jnp.dot(probs, v, preferred_element_type=jnp.float32)
            attended_ref[here, lanes] = unstacked_pair(o).astype(jnp.bfloat16)
        return carry

    lax.fori_loop(0, block_count, one_block, 0)

    @pl.when(edge_ref[0] == 0)
    def _():
        attended_ref[:BLOCK] = ends_ref[:BLOCK]

    @pl.when(edge_ref[0] + block_count == edge_ref[1])
    def _():
        attended_ref[row_count - BLOCK :] = ends_ref[BLOCK:]

    encoded = x_ref[...].astype(jnp.float32) + attended_ref[...].astype(jnp.float32)
    rows_ref[:row_count] = encoded.astype(jnp.bfloat16)
    project(rows_ref.at[:row_count], w_cross_ref, kv_ref.at[:row_count], 2 * BLOCK)
    partial_attention(sq_ref, kv_ref.at[:row_count], out_ref, log_ref)


def block_attention(ids, edge, everything, q, x, w_kv, w_cross, ends, sq, pick_count):
    slots = ids.shape[0]
    features = x.shape[1]
    return pl.pallas_call(
        functools.partial(block_kernel, pick_count),
        out_shape=[
            jax.ShapeDtypeStruct(q.shape, jnp.bfloat16),
            jax.ShapeDtypeStruct(sq.shape, jnp.bfloat16),
            jax.ShapeDtypeStruct((sq.shape[0], LANES), jnp.float32),
        ],
        in_specs=[SMEM, SMEM, ANY] + [VMEM] * 6,
        out_specs=[VMEM] * 3,
        scratch_shapes=[
            pltpu.VMEM((slots * BLOCK, features), jnp.bfloat16),
            pltpu.VMEM((slots * BLOCK, 2 * features), jnp.bfloat16),
            pltpu.SemaphoreType.DMA((slots,)),
        ],
        compiler_params=pltpu.CompilerParams(vmem_limit_bytes=VMEM_LIMIT),
        cost_estimate=pl.CostEstimate(
            flops=20 << 30, bytes_accessed=16 << 20, transcendentals=5 << 20
        ),
        name="block_attention",
    )(ids, edge, everything, q, x, w_kv, w_cross, ends, sq)


def combined(outs, logs):
    n, rows, features = outs.shape
    logs = logs[:, :, :HEADS]
    weights = jnp.exp(logs - jnp.max(logs, axis=0, keepdims=True))
    weights = weights / jnp.sum(weights, axis=0, keepdims=True)
    spread = jnp.broadcast_to(weights[:, :, :, None], (n, rows, HEADS, HEAD))
    spread = spread.reshape(n, rows, features)
    return jnp.sum(outs.astype(jnp.float32) * spread, axis=0).astype(jnp.bfloat16)


def dealt(x, n, each):
    x = jnp.pad(x, ((0, n * each - x.shape[0]), (0, 0)))
    return x.reshape(n, each, x.shape[1])


def local(queries, inputs, w_kv, rand_blocks, w_cross, vocab_table, summary_ids):
    n = lax.axis_size("ctx")
    position = lax.axis_index("ctx")
    row_count, features = inputs.shape
    block_count = row_count // BLOCK
    pick_count = rand_blocks.shape[1]
    total_blocks = block_count * n
    shard_rows = vocab_table.shape[0]
    summary_count = summary_ids.shape[0]
    share = summary_count // n
    each = -(-BLOCK // n)

    everything = lax.all_gather(inputs, "ctx", axis=0, tiled=True)
    everything = everything.reshape(total_blocks, BLOCK, features)

    offsets = summary_ids - position * shard_rows
    inside = jnp.logical_and(offsets >= 0, offsets < shard_rows)
    looked = vocab_table[jnp.clip(offsets, 0, shard_rows - 1)]
    looked = jnp.where(inside[:, None], looked, jnp.zeros((), looked.dtype))
    message = jnp.concatenate(
        [
            looked.reshape(n, share, features),
            dealt(queries[:BLOCK], n, each),
            dealt(queries[row_count - BLOCK :], n, each),
        ],
        axis=1,
    )
    (received,) = exchange([message], 1)
    mine = jnp.concatenate(
        [
            jnp.sum(received[:, :share].astype(jnp.float32), axis=0).astype(jnp.bfloat16),
            received[0, share : share + each],
            received[n - 1, share + each :],
        ],
        axis=0,
    )
    (rows,) = exchange([mine], 2, same=True)
    summary_queries = rows[:, :share].reshape(summary_count, features)
    first = rows[:, share : share + each].reshape(n * each, features)[:BLOCK]
    last = rows[:, share + each :].reshape(n * each, features)[:BLOCK]
    end_out, end_log = global_partial(jnp.concatenate([first, last], axis=0), inputs, w_kv)

    def split(x):
        return jnp.concatenate([dealt(x[:BLOCK], n, each), dealt(x[BLOCK:], n, each)], axis=1)

    got_out, got_log = exchange([split(end_out), split(end_log)], 3)
    (ends,) = exchange([combined(got_out, got_log)], 4, same=True)
    ends = jnp.concatenate(
        [
            ends[:, :each].reshape(n * each, features)[:BLOCK],
            ends[:, each:].reshape(n * each, features)[:BLOCK],
        ],
        axis=0,
    )

    start = position * block_count
    near = jnp.clip(start - 1 + jnp.arange(block_count + 2, dtype=jnp.int32), 0, total_blocks - 1)
    fixed = jnp.array([0, total_blocks - 1], jnp.int32)
    picks = lax.dynamic_slice_in_dim(rand_blocks, start, block_count, 0).reshape(-1)
    ids = jnp.concatenate([near, fixed, picks.astype(jnp.int32)])
    edge = jnp.stack([start, jnp.full_like(start, total_blocks)]).astype(jnp.int32)
    attended, part, logs = block_attention(
        ids, edge, everything, queries, inputs, w_kv, w_cross, ends, summary_queries, pick_count
    )
    parts, all_logs = exchange(
        [part.reshape(n, share, features), logs.reshape(n, share, LANES)], 5
    )
    return attended, combined(parts, all_logs)


def solution(mesh):
    return jax.shard_map(
        local,
        mesh=mesh,
        in_specs=(
            P(("groups", "ctx"), None),
            P(("groups", "ctx"), None),
            P(),
            P("groups", None),
            P(),
            P("ctx", None),
            P("groups"),
        ),
        out_specs=(P(("groups", "ctx"), None), P(("groups", "ctx"), None)),
        check_vma=False,
    )
```

```python
import functools

import jax
import jax.numpy as jnp
from jax import lax
from jax.experimental import pallas as pl
from jax.experimental.pallas import tpu as pltpu
from jax.sharding import PartitionSpec as P

HEADS = 16
HEAD = 64
BLOCK = 64
LANES = 128
PAIRS = HEADS // 2
MASKED_SCORE = -1e30
MESH = pl.DeviceIdType.MESH
VMEM = pl.BlockSpec(memory_space=pltpu.VMEM)
ANY = pl.BlockSpec(memory_space=pl.ANY)
SMEM = pl.BlockSpec(memory_space=pltpu.SMEM)
VMEM_LIMIT = 48 * 1024 * 1024


def greet_all(me, n):
    barrier = pltpu.get_barrier_semaphore()

    def greet(k, carry):
        peer = lax.rem(me + k, n)
        pl.semaphore_signal(barrier, inc=1, device_id={"ctx": peer}, device_id_type=MESH)
        return carry

    lax.fori_loop(1, n, greet, 0)
    pl.semaphore_wait(barrier, n - 1)


def push(source, target, send_sem, recv_sem, peer):
    return pltpu.make_async_remote_copy(
        source, target, send_sem, recv_sem, device_id={"ctx": peer}, device_id_type=MESH
    )


def each_peer(me, n, body):
    def step(k, carry):
        body(lax.rem(me + k, n))
        return carry

    lax.fori_loop(1, n, step, 0)


def gather_kernel(
    n,
    x_ref,
    q_ref,
    looked_ref,
    all_ref,
    ends_ref,
    got_ref,
    ring_send,
    ring_recv,
    side_send,
    side_recv,
    got_send,
    got_recv,
    ends_send,
    ends_recv,
    own_sem,
):
    me = lax.axis_index("ctx")
    chips = n // 2
    half = chips // 2
    core = me % 2
    chip = me // 2
    odd = chip % 2
    place = (1 - odd) * (chip // 2) + odd * (chips - 1 - chip // 2)
    sibling = me + 1 - 2 * core
    row_count = q_ref.shape[0]

    def device(at, on_core):
        at = (at + chips) % chips
        back = at // half
        return 2 * ((1 - back) * 2 * at + back * (2 * (chips - 1 - at) + 1)) + on_core

    streams = [(d, h) for h in range(2) for d in range(2)]

    def hops(d, h):
        return half if d == h else half - 1

    def ring(d, h, s):
        sign = 1 - 2 * d
        owner = device(place - sign * s, core)
        source = x_ref.at[h] if s == 0 else all_ref.at[owner, h]
        return push(
            source,
            all_ref.at[owner, h],
            ring_send.at[d, h, s],
            ring_recv.at[d, h, s],
            device(place + sign, core),
        )

    def arrival(d, h, s):
        owner = device(place - (1 - 2 * d) * (s + 1), core)
        landed = all_ref.at[owner, h]
        return push(landed, landed, ring_send.at[d, h, s], ring_recv.at[d, h, s], sibling)

    def side(d, h, s, on_core):
        owner = device(place - (1 - 2 * d) * s, on_core)
        source = all_ref.at[owner, h]
        if s == 0:
            source = x_ref.at[h]
        return push(
            source, all_ref.at[owner, h], side_send.at[d, h, s], side_recv.at[d, h, s], sibling
        )

    own = [pltpu.make_async_copy(x_ref.at[h], all_ref.at[me, h], own_sem.at[h]) for h in range(2)]
    own.append(pltpu.make_async_copy(looked_ref.at[me], got_ref.at[me], own_sem.at[2]))
    greet_all(me, n)
    for d, h in streams:
        ring(d, h, 0).start()

    def send_looked(peer):
        push(
            looked_ref.at[peer], got_ref.at[me], got_send.at[peer], got_recv.at[me], peer
        ).start()

    each_peer(me, n, send_looked)
    ends = [q_ref.at[pl.ds(0, BLOCK)], q_ref.at[pl.ds(row_count - BLOCK, BLOCK)]]
    holders = [0, n - 1]

    def send_end(e, peer):
        return push(
            ends[e], ends_ref.at[e], ends_send.at[e, peer], ends_recv.at[e], peer
        )

    for e in range(2):

        @pl.when(me == holders[e])
        def _():
            each_peer(me, n, lambda peer: send_end(e, peer).start())
            copy = pltpu.make_async_copy(ends[e], ends_ref.at[e], own_sem.at[3])
            copy.start()
            copy.wait()

    for copy in own:
        copy.start()
    for h in range(2):
        side(0, h, 0, core).start()
    for s in range(half):
        for d, h in streams:
            if s < hops(d, h):
                arrival(d, h, s).wait_recv()
                if s + 1 < hops(d, h):
                    ring(d, h, s + 1).start()
                side(d, h, s + 1, core).start()
    for h in range(2):
        side(0, h, 0, core).wait_send()
        side(0, h, 0, 1 - core).wait_recv()
    for s in range(half):
        for d, h in streams:
            if s < hops(d, h):
                ring(d, h, s).wait_send()
                side(d, h, s + 1, core).wait_send()
                side(d, h, s + 1, 1 - core).wait_recv()

    def end_looked(peer):
        copy = push(
            looked_ref.at[peer], got_ref.at[peer], got_send.at[peer], got_recv.at[peer], peer
        )
        copy.wait_recv()
        copy.wait_send()

    each_peer(me, n, end_looked)
    for e in range(2):

        @pl.when(me == holders[e])
        def _():
            each_peer(me, n, lambda peer: send_end(e, peer).wait_send())

        @pl.when(me != holders[e])
        def _():
            send_end(e, sibling).wait_recv()

    for copy in own:
        copy.wait()


def gather_inputs(x, q, looked):
    n = lax.axis_size("ctx")
    rows, features = x.shape
    half = n // 4
    dma = pltpu.SemaphoreType.DMA
    gathered, ends, got = pl.pallas_call(
        functools.partial(gather_kernel, n),
        out_shape=[
            jax.ShapeDtypeStruct((n, 2, rows // 2, features), x.dtype),
            jax.ShapeDtypeStruct((2, BLOCK, features), q.dtype),
            jax.ShapeDtypeStruct(looked.shape, looked.dtype),
        ],
        in_specs=[ANY] * 3,
        out_specs=[ANY] * 3,
        scratch_shapes=[
            dma((2, 2, half)),
            dma((2, 2, half)),
            dma((2, 2, half + 1)),
            dma((2, 2, half + 1)),
            dma((n,)),
            dma((n,)),
            dma((2, n)),
            dma((2,)),
            dma((4,)),
        ],
        compiler_params=pltpu.CompilerParams(collective_id=1, has_side_effects=True),
        name="gather_inputs",
    )(x.reshape(2, rows // 2, features), q, looked)
    return gathered.reshape(n * rows // BLOCK, BLOCK, features), ends, got


def ends_kernel(
    n,
    mine_ref,
    out_ref,
    log_ref,
    rows_ref,
    outs_ref,
    logs_ref,
    rows_send,
    rows_recv,
    ends_send,
    ends_recv,
    own_sem,
):
    me = lax.axis_index("ctx")
    holders = [0, n - 1]
    pairs = [(out_ref, outs_ref), (log_ref, logs_ref)]

    def end(e, i, slot):
        source, target = pairs[i]
        return push(
            source.at[e], target.at[slot], ends_send.at[e, i], ends_recv.at[i, slot], holders[e]
        )

    own = pltpu.make_async_copy(mine_ref, rows_ref.at[me], own_sem.at[2])
    own.start()
    greet_all(me, n)
    for e in range(2):

        @pl.when(me != holders[e])
        def _():
            for i in range(2):
                end(e, i, me).start()

        @pl.when(me == holders[e])
        def _():
            for i in range(2):
                source, target = pairs[i]
                copy = pltpu.make_async_copy(source.at[e], target.at[me], own_sem.at[i])
                copy.start()
                copy.wait()

    def send_rows(peer):
        push(mine_ref, rows_ref.at[me], rows_send.at[peer], rows_recv.at[me], peer).start()

    each_peer(me, n, send_rows)

    def end_rows(peer):
        copy = push(mine_ref, rows_ref.at[peer], rows_send.at[peer], rows_recv.at[peer], peer)
        copy.wait_recv()
        copy.wait_send()

    each_peer(me, n, end_rows)
    for e in range(2):

        @pl.when(me != holders[e])
        def _():
            for i in range(2):
                end(e, i, me).wait_send()

        @pl.when(me == holders[e])
        def _():
            def arrived(peer):
                for i in range(2):
                    source, target = pairs[i]
                    push(
                        source.at[e],
                        target.at[peer],
                        ends_send.at[e, i],
                        ends_recv.at[i, peer],
                        peer,
                    ).wait_recv()

            each_peer(me, n, arrived)

    own.wait()


def send_ends(mine, out, log):
    n = lax.axis_size("ctx")
    dma = pltpu.SemaphoreType.DMA
    out = out.reshape(2, BLOCK, out.shape[1])
    log = log.reshape(2, BLOCK, LANES)
    return pl.pallas_call(
        functools.partial(ends_kernel, n),
        out_shape=[
            jax.ShapeDtypeStruct((n,) + mine.shape, mine.dtype),
            jax.ShapeDtypeStruct((n,) + out.shape[1:], out.dtype),
            jax.ShapeDtypeStruct((n,) + log.shape[1:], log.dtype),
        ],
        in_specs=[ANY] * 3,
        out_specs=[ANY] * 3,
        scratch_shapes=[dma((n,)), dma((n,)), dma((2, 2)), dma((2, n)), dma((3,))],
        compiler_params=pltpu.CompilerParams(collective_id=2, has_side_effects=True),
        name="send_ends",
    )(mine, out, log)


def combine(outs_ref, logs_ref, total_ref):
    n, rows, features = outs_ref.shape
    peak = lax.fori_loop(
        1, n, lambda i, peak: jnp.maximum(peak, logs_ref[i]), logs_ref[0]
    )
    left = lax.broadcasted_iota(jnp.int32, (rows, LANES), 1) < HEAD
    total_ref[...] = jnp.zeros_like(total_ref)

    def spread(x, p):
        return jnp.where(left, x[:, 2 * p : 2 * p + 1], x[:, 2 * p + 1 : 2 * p + 2])

    def add(i, total):
        weights = jnp.exp(logs_ref[i] - peak)
        for p in range(PAIRS):
            lanes = slice(p * LANES, (p + 1) * LANES)
            total_ref[:, lanes] += outs_ref[i, :, lanes].astype(jnp.float32) * spread(weights, p)
        return total + weights

    scale = 1.0 / lax.fori_loop(0, n, add, jnp.zeros((rows, LANES), jnp.float32))
    for p in range(PAIRS):
        lanes = slice(p * LANES, (p + 1) * LANES)
        total_ref[:, lanes] = total_ref[:, lanes] * spread(scale, p)


def summary_kernel(
    n,
    part_ref,
    log_ref,
    out_ref,
    outs_ref,
    logs_ref,
    total_ref,
    send_sem,
    recv_sem,
    own_sem,
):
    me = lax.axis_index("ctx")
    pairs = [(part_ref, outs_ref), (log_ref, logs_ref)]
    own = [
        pltpu.make_async_copy(source.at[me], target.at[me], own_sem.at[i])
        for i, (source, target) in enumerate(pairs)
    ]
    for copy in own:
        copy.start()
    greet_all(me, n)

    def copies(peer, slot):
        return [
            push(
                source.at[peer], target.at[slot], send_sem.at[i, peer], recv_sem.at[i, slot], peer
            )
            for i, (source, target) in enumerate(pairs)
        ]

    def send(peer):
        for copy in copies(peer, me):
            copy.start()

    each_peer(me, n, send)

    def finish(peer):
        for copy in copies(peer, peer):
            copy.wait_recv()
            copy.wait_send()

    each_peer(me, n, finish)
    for copy in own:
        copy.wait()
    combine(outs_ref, logs_ref, total_ref)
    out_ref[...] = total_ref[...].astype(out_ref.dtype)


def combined_summary(part, logs):
    n, share, features = part.shape
    dma = pltpu.SemaphoreType.DMA
    return pl.pallas_call(
        functools.partial(summary_kernel, n),
        out_shape=jax.ShapeDtypeStruct((share, features), jnp.bfloat16),
        in_specs=[ANY] * 2,
        out_specs=VMEM,
        scratch_shapes=[
            pltpu.VMEM(part.shape, part.dtype),
            pltpu.VMEM(logs.shape, logs.dtype),
            pltpu.VMEM((share, features), jnp.float32),
            dma((2, n)),
            dma((2, n)),
            dma((2,)),
        ],
        compiler_params=pltpu.CompilerParams(collective_id=3, has_side_effects=True),
        name="combined_summary",
    )(part, logs)


def dot_t(a, b):
    return lax.dot_general(a, b, (((1,), (1,)), ((), ())), preferred_element_type=jnp.float32)


def stacked_pair(q):
    q = q * jnp.asarray(HEAD**-0.5, q.dtype)
    left = lax.broadcasted_iota(jnp.int32, q.shape, 1) < HEAD
    zero = jnp.zeros_like(q)
    return jnp.concatenate([jnp.where(left, q, zero), jnp.where(left, zero, q)], axis=0)


def unstacked_pair(o):
    rows = o.shape[0] // 2
    left = lax.broadcasted_iota(jnp.int32, (rows, LANES), 1) < HEAD
    return jnp.where(left, o[:rows], o[rows:])


def project(x_ref, w_ref, out_ref, tile):
    rows, cols = out_ref.shape
    width = 512

    def step(t, carry):
        at = pl.ds(pl.multiple_of(t * tile, tile), tile)
        x = x_ref[at, :]
        for c in range(cols // width):
            y = jnp.dot(
                x, w_ref[:, c * width : (c + 1) * width], preferred_element_type=jnp.float32
            )
            out_ref[at, c * width : (c + 1) * width] = y.astype(out_ref.dtype)
        return carry

    lax.fori_loop(0, rows // tile, step, 0)


def partial_attention(q_ref, kv_ref, out_ref, log_ref):
    rows, features = q_ref.shape
    place = lax.broadcasted_iota(jnp.int32, (rows, LANES), 1)
    logs = jnp.zeros((rows, LANES), jnp.float32)
    for p in range(PAIRS):
        lanes = slice(p * LANES, (p + 1) * LANES)
        values = slice(features + p * LANES, features + (p + 1) * LANES)
        scores = dot_t(stacked_pair(q_ref[:, lanes]), kv_ref[:, lanes])
        peak = jnp.max(scores, axis=1, keepdims=True)
        weights = jnp.exp(scores - peak)
        totals = jnp.sum(weights, axis=1, keepdims=True)
        sums = jnp.dot(
            weights.astype(jnp.bfloat16), kv_ref[:, values], preferred_element_type=jnp.float32
        )
        out_ref[:, lanes] = unstacked_pair(sums / totals).astype(out_ref.dtype)
        log = peak + jnp.log(totals)
        logs = jnp.where(place == 2 * p, log[:rows], logs)
        logs = jnp.where(place == 2 * p + 1, log[rows:], logs)
    log_ref[...] = logs


def global_kernel(q_ref, x_ref, w_ref, out_ref, log_ref, kv_ref):
    project(x_ref, w_ref, kv_ref, 128)
    partial_attention(q_ref, kv_ref, out_ref, log_ref)


def global_partial(q, x, w):
    return pl.pallas_call(
        global_kernel,
        out_shape=[
            jax.ShapeDtypeStruct(q.shape, jnp.bfloat16),
            jax.ShapeDtypeStruct((q.shape[0], LANES), jnp.float32),
        ],
        in_specs=[VMEM] * 3,
        out_specs=[VMEM] * 2,
        scratch_shapes=[pltpu.VMEM((x.shape[0], w.shape[1]), jnp.bfloat16)],
        compiler_params=pltpu.CompilerParams(vmem_limit_bytes=VMEM_LIMIT),
        cost_estimate=pl.CostEstimate(
            flops=2 * x.size * w.shape[1], bytes_accessed=6 << 20, transcendentals=1 << 20
        ),
        name="global_partial",
    )(q, x, w)


def block_kernel(
    pick_count,
    ids_ref,
    edge_ref,
    all_ref,
    q_ref,
    x_ref,
    w_kv_ref,
    w_cross_ref,
    outs_ref,
    logs_ref,
    sq_ref,
    attended_ref,
    out_ref,
    log_ref,
    rows_ref,
    kv_ref,
    total_ref,
    sem,
):
    row_count, features = x_ref.shape
    block_count = row_count // BLOCK
    slots = rows_ref.shape[0] // BLOCK
    far_start = (block_count + 4) * BLOCK
    span = (5 + pick_count) * BLOCK

    def fetch(i):
        return pltpu.make_async_copy(
            all_ref.at[ids_ref[i]],
            rows_ref.at[pl.ds(pl.multiple_of(i * BLOCK, BLOCK), BLOCK)],
            sem.at[i],
        )

    for i in range(slots):
        fetch(i).start()
    for i in range(slots):
        fetch(i).wait()
    project(rows_ref, w_kv_ref, kv_ref, 2 * BLOCK)

    column = lax.broadcasted_iota(jnp.int32, (2 * BLOCK, span), 1)

    def one_block(b, carry):
        first = edge_ref[0] + b
        hidden = jnp.logical_or(
            jnp.logical_and(column < BLOCK, first < 2),
            jnp.logical_and(
                jnp.logical_and(column >= 2 * BLOCK, column < 3 * BLOCK), first > edge_ref[1] - 3
            ),
        )
        near = pl.ds(pl.multiple_of(b * BLOCK, BLOCK), 3 * BLOCK)
        ends = pl.ds((block_count + 2) * BLOCK, 2 * BLOCK)
        far = pl.ds(
            pl.multiple_of(far_start + b * pick_count * BLOCK, BLOCK), pick_count * BLOCK
        )
        here = pl.ds(pl.multiple_of(b * BLOCK, BLOCK), BLOCK)
        for p in range(PAIRS):
            lanes = slice(p * LANES, (p + 1) * LANES)
            values = slice(features + p * LANES, features + (p + 1) * LANES)
            k = jnp.concatenate(
                [kv_ref[near, lanes], kv_ref[ends, lanes], kv_ref[far, lanes]], axis=0
            )
            v = jnp.concatenate(
                [kv_ref[near, values], kv_ref[ends, values], kv_ref[far, values]], axis=0
            )
            scores = dot_t(stacked_pair(q_ref[here, lanes]), k)
            scores = jnp.where(hidden, MASKED_SCORE, scores)
            weights = jnp.exp(scores - jnp.max(scores, axis=1, keepdims=True))
            totals = jnp.sum(weights, axis=1, keepdims=True)
            probs = (weights * (1.0 / totals)).astype(jnp.bfloat16)
            o = jnp.dot(probs, v, preferred_element_type=jnp.float32)
            attended_ref[here, lanes] = unstacked_pair(o).astype(jnp.bfloat16)
        return carry

    lax.fori_loop(0, block_count, one_block, 0)

    def place(rows):
        combine(outs_ref, logs_ref, total_ref)
        attended_ref[rows] = total_ref[...].astype(jnp.bfloat16)

    @pl.when(edge_ref[0] == 0)
    def _():
        place(slice(0, BLOCK))

    @pl.when(edge_ref[0] + block_count == edge_ref[1])
    def _():
        place(slice(row_count - BLOCK, row_count))

    encoded = x_ref[...].astype(jnp.float32) + attended_ref[...].astype(jnp.float32)
    rows_ref[:row_count] = encoded.astype(jnp.bfloat16)
    project(rows_ref.at[:row_count], w_cross_ref, kv_ref.at[:row_count], 2 * BLOCK)
    partial_attention(sq_ref, kv_ref.at[:row_count], out_ref, log_ref)


def block_attention(ids, edge, everything, q, x, w_kv, w_cross, outs, end_logs, sq, pick_count):
    slots = ids.shape[0]
    features = x.shape[1]
    return pl.pallas_call(
        functools.partial(block_kernel, pick_count),
        out_shape=[
            jax.ShapeDtypeStruct(q.shape, jnp.bfloat16),
            jax.ShapeDtypeStruct(sq.shape, jnp.bfloat16),
            jax.ShapeDtypeStruct((sq.shape[0], LANES), jnp.float32),
        ],
        in_specs=[SMEM, SMEM, ANY] + [VMEM] * 7,
        out_specs=[VMEM] * 3,
        scratch_shapes=[
            pltpu.VMEM((slots * BLOCK, features), jnp.bfloat16),
            pltpu.VMEM((slots * BLOCK, 2 * features), jnp.bfloat16),
            pltpu.VMEM((BLOCK, features), jnp.float32),
            pltpu.SemaphoreType.DMA((slots,)),
        ],
        compiler_params=pltpu.CompilerParams(vmem_limit_bytes=VMEM_LIMIT),
        cost_estimate=pl.CostEstimate(
            flops=20 << 30, bytes_accessed=16 << 20, transcendentals=5 << 20
        ),
        name="block_attention",
    )(ids, edge, everything, q, x, w_kv, w_cross, outs, end_logs, sq)


def local(queries, inputs, w_kv, rand_blocks, w_cross, vocab_table, summary_ids):
    n = lax.axis_size("ctx")
    position = lax.axis_index("ctx")
    row_count, features = inputs.shape
    block_count = row_count // BLOCK
    pick_count = rand_blocks.shape[1]
    total_blocks = block_count * n
    shard_rows = vocab_table.shape[0]
    summary_count = summary_ids.shape[0]
    share = summary_count // n
    offsets = summary_ids - position * shard_rows
    inside = jnp.logical_and(offsets >= 0, offsets < shard_rows)
    looked = vocab_table[jnp.clip(offsets, 0, shard_rows - 1)]
    looked = jnp.where(inside[:, None], looked, jnp.zeros((), looked.dtype))
    everything, end_queries, got = gather_inputs(
        inputs, queries, looked.reshape(n, share, features)
    )
    mine = jnp.sum(got.astype(jnp.float32), axis=0).astype(jnp.bfloat16)
    end_out, end_log = global_partial(end_queries.reshape(2 * BLOCK, features), inputs, w_kv)
    rows, outs, end_logs = send_ends(mine, end_out, end_log)
    summary_queries = rows.reshape(summary_count, features)

    start = position * block_count
    near = jnp.clip(start - 1 + jnp.arange(block_count + 2, dtype=jnp.int32), 0, total_blocks - 1)
    fixed = jnp.array([0, total_blocks - 1], jnp.int32)
    picks = lax.dynamic_slice_in_dim(rand_blocks, start, block_count, 0).reshape(-1)
    ids = jnp.concatenate([near, fixed, picks.astype(jnp.int32)])
    edge = jnp.stack([start, jnp.full_like(start, total_blocks)]).astype(jnp.int32)
    attended, part, logs = block_attention(
        ids,
        edge,
        everything,
        queries,
        inputs,
        w_kv,
        w_cross,
        outs,
        end_logs,
        summary_queries,
        pick_count,
    )
    summary = combined_summary(
        part.reshape(n, share, features), logs.reshape(n, share, LANES)
    )
    return attended, summary


def solution(mesh):
    return jax.shard_map(
        local,
        mesh=mesh,
        in_specs=(
            P(("groups", "ctx"), None),
            P(("groups", "ctx"), None),
            P(),
            P("groups", None),
            P(),
            P("ctx", None),
            P("groups"),
        ),
        out_specs=(P(("groups", "ctx"), None), P(("groups", "ctx"), None)),
        check_vma=False,
    )
```

```python
import functools

import jax
import jax.numpy as jnp
from jax import lax
from jax.experimental import pallas as pl
from jax.experimental.pallas import tpu as pltpu
from jax.sharding import PartitionSpec as P

HEADS = 16
HEAD = 64
BLOCK = 64
LANES = 128
PAIRS = HEADS // 2
MASKED_SCORE = -1e30
MESH = pl.DeviceIdType.MESH
VMEM = pl.BlockSpec(memory_space=pltpu.VMEM)
ANY = pl.BlockSpec(memory_space=pl.ANY)
SMEM = pl.BlockSpec(memory_space=pltpu.SMEM)
VMEM_LIMIT = 48 * 1024 * 1024


def greet_all(me, n):
    barrier = pltpu.get_barrier_semaphore()

    def greet(k, carry):
        peer = lax.rem(me + k, n)
        pl.semaphore_signal(barrier, inc=1, device_id={"ctx": peer}, device_id_type=MESH)
        return carry

    lax.fori_loop(1, n, greet, 0)
    pl.semaphore_wait(barrier, n - 1)


def push(source, target, send_sem, recv_sem, peer):
    return pltpu.make_async_remote_copy(
        source, target, send_sem, recv_sem, device_id={"ctx": peer}, device_id_type=MESH
    )


def each_peer(me, n, body):
    def step(k, carry):
        body(lax.rem(me + k, n))
        return carry

    lax.fori_loop(1, n, step, 0)


def gather_kernel(
    n,
    x_ref,
    q_ref,
    looked_ref,
    all_ref,
    ends_ref,
    got_ref,
    ring_send,
    ring_recv,
    side_send,
    side_recv,
    got_send,
    got_recv,
    ends_send,
    ends_recv,
    own_sem,
):
    me = lax.axis_index("ctx")
    chips = n // 2
    half = chips // 2
    core = me % 2
    chip = me // 2
    odd = chip % 2
    place = (1 - odd) * (chip // 2) + odd * (chips - 1 - chip // 2)
    sibling = me + 1 - 2 * core
    row_count = q_ref.shape[0]

    def device(at, on_core):
        at = (at + chips) % chips
        back = at // half
        return 2 * ((1 - back) * 2 * at + back * (2 * (chips - 1 - at) + 1)) + on_core

    streams = [(d, h) for h in range(2) for d in range(2)]

    def hops(d, h):
        return half if d == h else half - 1

    def ring(d, h, s):
        sign = 1 - 2 * d
        owner = device(place - sign * s, core)
        source = x_ref.at[h] if s == 0 else all_ref.at[owner, h]
        return push(
            source,
            all_ref.at[owner, h],
            ring_send.at[d, h, s],
            ring_recv.at[d, h, s],
            device(place + sign, core),
        )

    def arrival(d, h, s):
        owner = device(place - (1 - 2 * d) * (s + 1), core)
        landed = all_ref.at[owner, h]
        return push(landed, landed, ring_send.at[d, h, s], ring_recv.at[d, h, s], sibling)

    def side(d, h, s, on_core):
        owner = device(place - (1 - 2 * d) * s, on_core)
        source = all_ref.at[owner, h]
        if s == 0:
            source = x_ref.at[h]
        return push(
            source, all_ref.at[owner, h], side_send.at[d, h, s], side_recv.at[d, h, s], sibling
        )

    own = [pltpu.make_async_copy(x_ref.at[h], all_ref.at[me, h], own_sem.at[h]) for h in range(2)]
    own.append(pltpu.make_async_copy(looked_ref.at[me], got_ref.at[me], own_sem.at[2]))
    greet_all(me, n)
    for d, h in streams:
        ring(d, h, 0).start()

    def send_looked(peer):
        push(
            looked_ref.at[peer], got_ref.at[me], got_send.at[peer], got_recv.at[me], peer
        ).start()

    each_peer(me, n, send_looked)
    ends = [q_ref.at[pl.ds(0, BLOCK)], q_ref.at[pl.ds(row_count - BLOCK, BLOCK)]]
    holders = [0, n - 1]

    steps = [(place - at + chips) % chips for at in (0, half)]
    right, left = device(place + 1, core), device(place - 1, core)

    def send_end(e, k, source):
        peer = (right, left, sibling)[k]
        return push(source, ends_ref.at[e], ends_send.at[e, k], ends_recv.at[e], peer)

    def routes(e):
        away = steps[e]
        return [
            (0, away < half),
            (1, jnp.logical_or(away == 0, away > chips - half + 1)),
            (2, me == holders[e]),
        ]

    def start_routes(e, source):
        for k, goes in routes(e)[:2]:

            @pl.when(goes)
            def _():
                send_end(e, k, source).start()

    def pass_end(e):
        send_end(e, 0, ends_ref.at[e]).wait_recv()
        start_routes(e, ends_ref.at[e])

    for e in range(2):

        @pl.when(me == holders[e])
        def _():
            send_end(e, 2, ends[e]).start()
            start_routes(e, ends[e])
            copy = pltpu.make_async_copy(ends[e], ends_ref.at[e], own_sem.at[3])
            copy.start()
            copy.wait()

        @pl.when(jnp.logical_and(steps[e] == 0, me != holders[e]))
        def _():
            pass_end(e)

    for copy in own:
        copy.start()
    for h in range(2):
        side(0, h, 0, core).start()
    for s in range(half):
        for d, h in streams:
            if s < hops(d, h):
                arrival(d, h, s).wait_recv()
                if s + 1 < hops(d, h):
                    ring(d, h, s + 1).start()
                side(d, h, s + 1, core).start()
        for e in range(2):
            near = steps[e] == s + 1
            if s + 1 < half:
                near = jnp.logical_or(near, steps[e] == chips - s - 1)

            @pl.when(near)
            def _():
                pass_end(e)

    for h in range(2):
        side(0, h, 0, core).wait_send()
        side(0, h, 0, 1 - core).wait_recv()
    for s in range(half):
        for d, h in streams:
            if s < hops(d, h):
                ring(d, h, s).wait_send()
                side(d, h, s + 1, core).wait_send()
                side(d, h, s + 1, 1 - core).wait_recv()

    def end_looked(peer):
        copy = push(
            looked_ref.at[peer], got_ref.at[peer], got_send.at[peer], got_recv.at[peer], peer
        )
        copy.wait_recv()
        copy.wait_send()

    each_peer(me, n, end_looked)
    for e in range(2):
        for k, goes in routes(e):

            @pl.when(goes)
            def _():
                send_end(e, k, ends[e]).wait_send()

    for copy in own:
        copy.wait()


def gather_inputs(x, q, looked):
    n = lax.axis_size("ctx")
    rows, features = x.shape
    half = n // 4
    dma = pltpu.SemaphoreType.DMA
    gathered, ends, got = pl.pallas_call(
        functools.partial(gather_kernel, n),
        out_shape=[
            jax.ShapeDtypeStruct((n, 2, rows // 2, features), x.dtype),
            jax.ShapeDtypeStruct((2, BLOCK, features), q.dtype),
            jax.ShapeDtypeStruct(looked.shape, looked.dtype),
        ],
        in_specs=[ANY] * 3,
        out_specs=[ANY] * 3,
        scratch_shapes=[
            dma((2, 2, half)),
            dma((2, 2, half)),
            dma((2, 2, half + 1)),
            dma((2, 2, half + 1)),
            dma((n,)),
            dma((n,)),
            dma((2, 3)),
            dma((2,)),
            dma((4,)),
        ],
        compiler_params=pltpu.CompilerParams(collective_id=1, has_side_effects=True),
        name="gather_inputs",
    )(x.reshape(2, rows // 2, features), q, looked)
    return gathered.reshape(n * rows // BLOCK, BLOCK, features), ends, got


def ends_kernel(
    n,
    mine_ref,
    out_ref,
    log_ref,
    rows_ref,
    outs_ref,
    logs_ref,
    rows_send,
    rows_recv,
    ends_send,
    ends_recv,
    own_sem,
):
    me = lax.axis_index("ctx")
    holders = [0, n - 1]
    pairs = [(out_ref, outs_ref), (log_ref, logs_ref)]

    def end(e, i, slot):
        source, target = pairs[i]
        return push(
            source.at[e], target.at[slot], ends_send.at[e, i], ends_recv.at[i, slot], holders[e]
        )

    own = pltpu.make_async_copy(mine_ref, rows_ref.at[me], own_sem.at[2])
    own.start()
    greet_all(me, n)
    for e in range(2):

        @pl.when(me != holders[e])
        def _():
            for i in range(2):
                end(e, i, me).start()

        @pl.when(me == holders[e])
        def _():
            for i in range(2):
                source, target = pairs[i]
                copy = pltpu.make_async_copy(source.at[e], target.at[me], own_sem.at[i])
                copy.start()
                copy.wait()

    def send_rows(peer):
        push(mine_ref, rows_ref.at[me], rows_send.at[peer], rows_recv.at[me], peer).start()

    each_peer(me, n, send_rows)

    def end_rows(peer):
        copy = push(mine_ref, rows_ref.at[peer], rows_send.at[peer], rows_recv.at[peer], peer)
        copy.wait_recv()
        copy.wait_send()

    each_peer(me, n, end_rows)
    for e in range(2):

        @pl.when(me != holders[e])
        def _():
            for i in range(2):
                end(e, i, me).wait_send()

        @pl.when(me == holders[e])
        def _():
            def arrived(peer):
                for i in range(2):
                    source, target = pairs[i]
                    push(
                        source.at[e],
                        target.at[peer],
                        ends_send.at[e, i],
                        ends_recv.at[i, peer],
                        peer,
                    ).wait_recv()

            each_peer(me, n, arrived)

    own.wait()


def send_ends(mine, out, log):
    n = lax.axis_size("ctx")
    dma = pltpu.SemaphoreType.DMA
    out = out.reshape(2, BLOCK, out.shape[1])
    log = log.reshape(2, BLOCK, LANES)
    return pl.pallas_call(
        functools.partial(ends_kernel, n),
        out_shape=[
            jax.ShapeDtypeStruct((n,) + mine.shape, mine.dtype),
            jax.ShapeDtypeStruct((n,) + out.shape[1:], out.dtype),
            jax.ShapeDtypeStruct((n,) + log.shape[1:], log.dtype),
        ],
        in_specs=[ANY] * 3,
        out_specs=[ANY] * 3,
        scratch_shapes=[dma((n,)), dma((n,)), dma((2, 2)), dma((2, n)), dma((3,))],
        compiler_params=pltpu.CompilerParams(collective_id=2, has_side_effects=True),
        name="send_ends",
    )(mine, out, log)


def combine(outs_ref, logs_ref, total_ref):
    n, rows, features = outs_ref.shape
    peak = lax.fori_loop(
        1, n, lambda i, peak: jnp.maximum(peak, logs_ref[i]), logs_ref[0]
    )
    left = lax.broadcasted_iota(jnp.int32, (rows, LANES), 1) < HEAD
    total_ref[...] = jnp.zeros_like(total_ref)

    def spread(x, p):
        return jnp.where(left, x[:, 2 * p : 2 * p + 1], x[:, 2 * p + 1 : 2 * p + 2])

    def add(i, total):
        weights = jnp.exp(logs_ref[i] - peak)
        for p in range(PAIRS):
            lanes = slice(p * LANES, (p + 1) * LANES)
            total_ref[:, lanes] += outs_ref[i, :, lanes].astype(jnp.float32) * spread(weights, p)
        return total + weights

    scale = 1.0 / lax.fori_loop(0, n, add, jnp.zeros((rows, LANES), jnp.float32))
    for p in range(PAIRS):
        lanes = slice(p * LANES, (p + 1) * LANES)
        total_ref[:, lanes] = total_ref[:, lanes] * spread(scale, p)


def summary_kernel(
    n,
    part_ref,
    log_ref,
    out_ref,
    outs_ref,
    logs_ref,
    total_ref,
    send_sem,
    recv_sem,
    own_sem,
):
    me = lax.axis_index("ctx")
    pairs = [(part_ref, outs_ref), (log_ref, logs_ref)]
    own = [
        pltpu.make_async_copy(source.at[me], target.at[me], own_sem.at[i])
        for i, (source, target) in enumerate(pairs)
    ]
    for copy in own:
        copy.start()
    greet_all(me, n)

    def copies(peer, slot):
        return [
            push(
                source.at[peer], target.at[slot], send_sem.at[i, peer], recv_sem.at[i, slot], peer
            )
            for i, (source, target) in enumerate(pairs)
        ]

    def send(peer):
        for copy in copies(peer, me):
            copy.start()

    each_peer(me, n, send)

    def finish(peer):
        for copy in copies(peer, peer):
            copy.wait_recv()
            copy.wait_send()

    each_peer(me, n, finish)
    for copy in own:
        copy.wait()
    combine(outs_ref, logs_ref, total_ref)
    out_ref[...] = total_ref[...].astype(out_ref.dtype)


def combined_summary(part, logs):
    n, share, features = part.shape
    dma = pltpu.SemaphoreType.DMA
    return pl.pallas_call(
        functools.partial(summary_kernel, n),
        out_shape=jax.ShapeDtypeStruct((share, features), jnp.bfloat16),
        in_specs=[ANY] * 2,
        out_specs=VMEM,
        scratch_shapes=[
            pltpu.VMEM(part.shape, part.dtype),
            pltpu.VMEM(logs.shape, logs.dtype),
            pltpu.VMEM((share, features), jnp.float32),
            dma((2, n)),
            dma((2, n)),
            dma((2,)),
        ],
        compiler_params=pltpu.CompilerParams(collective_id=3, has_side_effects=True),
        name="combined_summary",
    )(part, logs)


def dot_t(a, b):
    return lax.dot_general(a, b, (((1,), (1,)), ((), ())), preferred_element_type=jnp.float32)


def stacked_pair(q):
    q = q * jnp.asarray(HEAD**-0.5, q.dtype)
    left = lax.broadcasted_iota(jnp.int32, q.shape, 1) < HEAD
    zero = jnp.zeros_like(q)
    return jnp.concatenate([jnp.where(left, q, zero), jnp.where(left, zero, q)], axis=0)


def unstacked_pair(o):
    rows = o.shape[0] // 2
    left = lax.broadcasted_iota(jnp.int32, (rows, LANES), 1) < HEAD
    return jnp.where(left, o[:rows], o[rows:])


def project(x_ref, w_ref, out_ref, tile):
    rows, cols = out_ref.shape
    width = 512

    def step(t, carry):
        at = pl.ds(pl.multiple_of(t * tile, tile), tile)
        x = x_ref[at, :]
        for c in range(cols // width):
            y = jnp.dot(
                x, w_ref[:, c * width : (c + 1) * width], preferred_element_type=jnp.float32
            )
            out_ref[at, c * width : (c + 1) * width] = y.astype(out_ref.dtype)
        return carry

    lax.fori_loop(0, rows // tile, step, 0)


def partial_attention(q_ref, kv_ref, out_ref, log_ref):
    rows, features = q_ref.shape
    place = lax.broadcasted_iota(jnp.int32, (rows, LANES), 1)
    logs = jnp.zeros((rows, LANES), jnp.float32)
    for p in range(PAIRS):
        lanes = slice(p * LANES, (p + 1) * LANES)
        values = slice(features + p * LANES, features + (p + 1) * LANES)
        scores = dot_t(stacked_pair(q_ref[:, lanes]), kv_ref[:, lanes])
        peak = jnp.max(scores, axis=1, keepdims=True)
        weights = jnp.exp(scores - peak)
        totals = jnp.sum(weights, axis=1, keepdims=True)
        sums = jnp.dot(
            weights.astype(jnp.bfloat16), kv_ref[:, values], preferred_element_type=jnp.float32
        )
        out_ref[:, lanes] = unstacked_pair(sums / totals).astype(out_ref.dtype)
        log = peak + jnp.log(totals)
        logs = jnp.where(place == 2 * p, log[:rows], logs)
        logs = jnp.where(place == 2 * p + 1, log[rows:], logs)
    log_ref[...] = logs


def global_kernel(q_ref, x_ref, w_ref, out_ref, log_ref, kv_ref):
    project(x_ref, w_ref, kv_ref, 128)
    partial_attention(q_ref, kv_ref, out_ref, log_ref)


def global_partial(q, x, w):
    return pl.pallas_call(
        global_kernel,
        out_shape=[
            jax.ShapeDtypeStruct(q.shape, jnp.bfloat16),
            jax.ShapeDtypeStruct((q.shape[0], LANES), jnp.float32),
        ],
        in_specs=[VMEM] * 3,
        out_specs=[VMEM] * 2,
        scratch_shapes=[pltpu.VMEM((x.shape[0], w.shape[1]), jnp.bfloat16)],
        compiler_params=pltpu.CompilerParams(vmem_limit_bytes=VMEM_LIMIT),
        cost_estimate=pl.CostEstimate(
            flops=2 * x.size * w.shape[1], bytes_accessed=6 << 20, transcendentals=1 << 20
        ),
        name="global_partial",
    )(q, x, w)


def block_kernel(
    pick_count,
    ids_ref,
    edge_ref,
    all_ref,
    q_ref,
    x_ref,
    w_kv_ref,
    w_cross_ref,
    outs_ref,
    logs_ref,
    sq_ref,
    attended_ref,
    out_ref,
    log_ref,
    rows_ref,
    kv_ref,
    total_ref,
    sem,
):
    row_count, features = x_ref.shape
    block_count = row_count // BLOCK
    slots = rows_ref.shape[0] // BLOCK
    far_start = (block_count + 4) * BLOCK
    span = (5 + pick_count) * BLOCK

    def fetch(i):
        return pltpu.make_async_copy(
            all_ref.at[ids_ref[i]],
            rows_ref.at[pl.ds(pl.multiple_of(i * BLOCK, BLOCK), BLOCK)],
            sem.at[i],
        )

    for i in range(slots):
        fetch(i).start()
    for i in range(slots):
        fetch(i).wait()
    project(rows_ref, w_kv_ref, kv_ref, 2 * BLOCK)

    column = lax.broadcasted_iota(jnp.int32, (2 * BLOCK, span), 1)

    def one_block(b, carry):
        first = edge_ref[0] + b
        hidden = jnp.logical_or(
            jnp.logical_and(column < BLOCK, first < 2),
            jnp.logical_and(
                jnp.logical_and(column >= 2 * BLOCK, column < 3 * BLOCK), first > edge_ref[1] - 3
            ),
        )
        near = pl.ds(pl.multiple_of(b * BLOCK, BLOCK), 3 * BLOCK)
        ends = pl.ds((block_count + 2) * BLOCK, 2 * BLOCK)
        far = pl.ds(
            pl.multiple_of(far_start + b * pick_count * BLOCK, BLOCK), pick_count * BLOCK
        )
        here = pl.ds(pl.multiple_of(b * BLOCK, BLOCK), BLOCK)
        for p in range(PAIRS):
            lanes = slice(p * LANES, (p + 1) * LANES)
            values = slice(features + p * LANES, features + (p + 1) * LANES)
            k = jnp.concatenate(
                [kv_ref[near, lanes], kv_ref[ends, lanes], kv_ref[far, lanes]], axis=0
            )
            v = jnp.concatenate(
                [kv_ref[near, values], kv_ref[ends, values], kv_ref[far, values]], axis=0
            )
            scores = dot_t(stacked_pair(q_ref[here, lanes]), k)
            scores = jnp.where(hidden, MASKED_SCORE, scores)
            weights = jnp.exp(scores - jnp.max(scores, axis=1, keepdims=True))
            totals = jnp.sum(weights, axis=1, keepdims=True)
            probs = (weights * (1.0 / totals)).astype(jnp.bfloat16)
            o = jnp.dot(probs, v, preferred_element_type=jnp.float32)
            attended_ref[here, lanes] = unstacked_pair(o).astype(jnp.bfloat16)
        return carry

    lax.fori_loop(0, block_count, one_block, 0)

    def place(rows):
        combine(outs_ref, logs_ref, total_ref)
        attended_ref[rows] = total_ref[...].astype(jnp.bfloat16)

    @pl.when(edge_ref[0] == 0)
    def _():
        place(slice(0, BLOCK))

    @pl.when(edge_ref[0] + block_count == edge_ref[1])
    def _():
        place(slice(row_count - BLOCK, row_count))

    encoded = x_ref[...].astype(jnp.float32) + attended_ref[...].astype(jnp.float32)
    rows_ref[:row_count] = encoded.astype(jnp.bfloat16)
    project(rows_ref.at[:row_count], w_cross_ref, kv_ref.at[:row_count], 2 * BLOCK)
    partial_attention(sq_ref, kv_ref.at[:row_count], out_ref, log_ref)


def block_attention(ids, edge, everything, q, x, w_kv, w_cross, outs, end_logs, sq, pick_count):
    slots = ids.shape[0]
    features = x.shape[1]
    return pl.pallas_call(
        functools.partial(block_kernel, pick_count),
        out_shape=[
            jax.ShapeDtypeStruct(q.shape, jnp.bfloat16),
            jax.ShapeDtypeStruct(sq.shape, jnp.bfloat16),
            jax.ShapeDtypeStruct((sq.shape[0], LANES), jnp.float32),
        ],
        in_specs=[SMEM, SMEM, ANY] + [VMEM] * 7,
        out_specs=[VMEM] * 3,
        scratch_shapes=[
            pltpu.VMEM((slots * BLOCK, features), jnp.bfloat16),
            pltpu.VMEM((slots * BLOCK, 2 * features), jnp.bfloat16),
            pltpu.VMEM((BLOCK, features), jnp.float32),
            pltpu.SemaphoreType.DMA((slots,)),
        ],
        compiler_params=pltpu.CompilerParams(vmem_limit_bytes=VMEM_LIMIT),
        cost_estimate=pl.CostEstimate(
            flops=20 << 30, bytes_accessed=16 << 20, transcendentals=5 << 20
        ),
        name="block_attention",
    )(ids, edge, everything, q, x, w_kv, w_cross, outs, end_logs, sq)


def local(queries, inputs, w_kv, rand_blocks, w_cross, vocab_table, summary_ids):
    n = lax.axis_size("ctx")
    position = lax.axis_index("ctx")
    row_count, features = inputs.shape
    block_count = row_count // BLOCK
    pick_count = rand_blocks.shape[1]
    total_blocks = block_count * n
    shard_rows = vocab_table.shape[0]
    summary_count = summary_ids.shape[0]
    share = summary_count // n
    offsets = summary_ids - position * shard_rows
    inside = jnp.logical_and(offsets >= 0, offsets < shard_rows)
    looked = vocab_table[jnp.clip(offsets, 0, shard_rows - 1)]
    looked = jnp.where(inside[:, None], looked, jnp.zeros((), looked.dtype))
    everything, end_queries, got = gather_inputs(
        inputs, queries, looked.reshape(n, share, features)
    )
    mine = jnp.sum(got.astype(jnp.float32), axis=0).astype(jnp.bfloat16)
    end_out, end_log = global_partial(end_queries.reshape(2 * BLOCK, features), inputs, w_kv)
    rows, outs, end_logs = send_ends(mine, end_out, end_log)
    summary_queries = rows.reshape(summary_count, features)

    start = position * block_count
    near = jnp.clip(start - 1 + jnp.arange(block_count + 2, dtype=jnp.int32), 0, total_blocks - 1)
    fixed = jnp.array([0, total_blocks - 1], jnp.int32)
    picks = lax.dynamic_slice_in_dim(rand_blocks, start, block_count, 0).reshape(-1)
    ids = jnp.concatenate([near, fixed, picks.astype(jnp.int32)])
    edge = jnp.stack([start, jnp.full_like(start, total_blocks)]).astype(jnp.int32)
    attended, part, logs = block_attention(
        ids,
        edge,
        everything,
        queries,
        inputs,
        w_kv,
        w_cross,
        outs,
        end_logs,
        summary_queries,
        pick_count,
    )
    summary = combined_summary(
        part.reshape(n, share, features), logs.reshape(n, share, LANES)
    )
    return attended, summary


def solution(mesh):
    return jax.shard_map(
        local,
        mesh=mesh,
        in_specs=(
            P(("groups", "ctx"), None),
            P(("groups", "ctx"), None),
            P(),
            P("groups", None),
            P(),
            P("ctx", None),
            P("groups"),
        ),
        out_specs=(P(("groups", "ctx"), None), P(("groups", "ctx"), None)),
        check_vma=False,
    )
```
